32 devices in a mesh: member: 2 (over core), grid: 16 (over z, y, x).
Axes of the slice: x: 2, y: 2, z: 4, core: 2. Of those that a mesh axis runs over, the one named last changes fastest.
Arguments:
- latent: bfloat16 [4, 32768, 512], P('member', 'grid'), may hold values from -80 to 80
- block_pick: int32 [16, 16], P('grid'), may hold values from 0 to 15
- obs_weight: bfloat16 [16, 16, 128, 128], P('grid'), may hold values from 0.0099487305 to 1
- obs_value: float32 [16, 16, 128, 128], P('grid'), may hold values from -6 to 6
- obs_count: int32 [16, 16], P('grid'), may hold values from 0 to 128, as said below
- w_in: bfloat16 [512, 512], replicated, may hold values from -0.25 to 0.25
- b_in: float32 [512], replicated, may hold values from -3 to 3
- w_out: bfloat16 [512, 128], replicated, may hold values from -0.25 to 0.25
- b_out: float32 [128], replicated, may hold values from -3 to 3
Outputs:
- latent_grad: float32 [4, 32768, 512], P('member', 'grid')
- loss_value: float32 [], replicated
The draws below stay inside these ranges and needn't reach their ends.
Inputs may be any that keep to these rules, and one draw needn't show every extreme that they name: Entry [d, j] counts the live observations of those slots; the live ones are the first slots, k < obs_count[d, j].
All inputs are finite; a program needn't handle non-finite values.
Results may differ from the reference program's by a relative error of at most 0.0041.
Values may be sent and summed in bfloat16 or wider, within the bound.
A program may use at most 128 MiB of HBM per device.

```python
import math
import jax
import jax.numpy as jnp
from jax import lax

WIDTH = 512
INNER_WIDTH = 512
OBS_CH = 128
BLOCK = 128
POINTS_DEV = 2048
MEMBERS = 4
POINTS = 32768
SLOTS = 128
OBS_ALL = 32768
N_GRID = 16


def draw_obs_count(key, part):
    row_index = jnp.arange(N_GRID, dtype=jnp.int32)
    capacity = jnp.maximum(SLOTS * (N_GRID + 2 * row_index) // (3 * N_GRID - 2), 1)
    lowest = capacity // 2
    spread = jax.random.randint(key, (N_GRID, N_GRID), 0, 1048576, dtype=jnp.int32)
    counts = lowest[:, None] + spread % (capacity - lowest + 1)[:, None]
    diagonal = row_index[:, None] == row_index[None, :]
    return jnp.where(diagonal, capacity[:, None], counts).astype(jnp.int32)


def draw_latent(key, part):
    member_pos = jnp.arange(MEMBERS, dtype=jnp.float32) / (MEMBERS - 1.0)
    sub_key = jax.random.fold_in(key, 7331)
    member_scale = 1.5 * jnp.power(8.0, member_pos)
    base = jnp.clip(jax.random.normal(sub_key, (MEMBERS, POINTS, WIDTH), jnp.float32), -6.0, 6.0)
    return (base * member_scale[:, None, None]).astype(jnp.bfloat16)


def set_ends(entries, rng, low, largest):
    longest = entries.shape.index(max(entries.shape))
    spots = []
    for shift in (0, 1):
        where = [jax.random.randint(jax.random.fold_in(rng, axis), (), 0, length) for axis, length in enumerate(entries.shape)]
        where[longest] = (where[longest] + shift) % entries.shape[longest]
        spots.append(tuple(where))
    return entries.at[spots[0]].set(low).at[spots[1]].set(largest)


def shard_levels(rng, dims, shards, low, largest):
    def one(position, shards_of):
        steps = jax.random.uniform(jax.random.fold_in(jax.random.fold_in(rng, 6), position), (shards_of,), jnp.float32, low / len(shards), largest / len(shards))
        return jnp.repeat(jnp.exp(steps), dims[position] // shards_of).reshape((-1,) + (1,) * (len(dims) - position - 1))

    loudness = one(*shards[0])
    for cut in shards[1:]:
        loudness = loudness * one(*cut)
    return loudness


def bell_draw(key, extent, width, limit, shards=(), held_as=jnp.bfloat16):
    entries = width * jax.random.normal(key, extent, jnp.float32)
    if shards:
        entries = entries * shard_levels(key, extent, shards, -0.22, 0.18)
    return jnp.clip(entries, -limit, limit).astype(held_as)


def setup_inputs(seed: int = 0) -> dict:
    streams_of = jax.random.split(jax.random.key(seed), 10)
    return {
        "latent": draw_latent(jax.random.fold_in(streams_of[9], 71), 0),
        "block_pick": set_ends(jax.random.randint(streams_of[1], (N_GRID, N_GRID), 0, POINTS_DEV // BLOCK), jax.random.fold_in(streams_of[1], 1), 0, (POINTS_DEV // BLOCK) - 1).astype(jnp.int32),
        "obs_weight": jnp.clip(jnp.exp(math.log(1.0) - 4.61031033 * jax.random.uniform(streams_of[2], (N_GRID, N_GRID, SLOTS, BLOCK), jnp.float32) ** shard_levels(streams_of[2], (N_GRID, N_GRID, SLOTS, BLOCK), ((0, 16),), -0.2, 0.2)), 0.0099487305, 1.0).astype(jnp.bfloat16),
        "obs_value": bell_draw(streams_of[3], (N_GRID, N_GRID, SLOTS, OBS_CH), 1.0, 6.0, ((0, 16),), jnp.float32),
        "obs_count": draw_obs_count(jax.random.fold_in(streams_of[9], 71), 0),
        "w_in": bell_draw(streams_of[5], (WIDTH, INNER_WIDTH), WIDTH ** -0.5, 0.25),
        "b_in": bell_draw(streams_of[6], (INNER_WIDTH,), 0.5, 3.0, (), jnp.float32),
        "w_out": bell_draw(streams_of[7], (INNER_WIDTH, OBS_CH), INNER_WIDTH ** -0.5, 0.25),
        "b_out": bell_draw(streams_of[8], (OBS_CH,), 0.5, 3.0, (), jnp.float32),
    }


SOFTEN = 0.1

def smooth_abs(value):
    return jnp.sqrt(value * value + SOFTEN * SOFTEN)

def silu_slope(pre_act):
    sigmoid_value = jax.nn.sigmoid(pre_act)
    return sigmoid_value * (1.0 + pre_act * (1.0 - sigmoid_value))

def reference(latent, block_pick, obs_weight, obs_value, obs_count, w_in, b_in, w_out, b_out):
    block_count = POINTS_DEV // BLOCK
    weight_sum = lax.optimization_barrier(jnp.sum(obs_weight.astype(jnp.float32), axis=3, keepdims=True))
    norm_weight = (obs_weight.astype(jnp.float32) / weight_sum).astype(jnp.bfloat16)
    live_mask = (jnp.arange(SLOTS, dtype=jnp.int32)[None, None, :] < obs_count[:, :, None]).astype(jnp.float32)
    local_blocks = latent.reshape(MEMBERS, N_GRID, block_count, BLOCK, WIDTH)
    owners = jnp.arange(N_GRID, dtype=jnp.int32)

    def forward(owner_index):
        owned = jnp.take(local_blocks, owner_index, axis=1)
        picked_ids = jnp.take(block_pick, owner_index, axis=0).astype(jnp.int32)
        picked = jnp.take(owned, picked_ids, axis=1)
        weights = jnp.take(norm_weight, owner_index, axis=1)
        interp = jnp.einsum('dkp,mdpc->mdkc', weights.astype(jnp.float32), picked.astype(jnp.float32)).astype(jnp.bfloat16)
        pre_act = jnp.einsum('mdkc,ch->mdkh', interp.astype(jnp.float32), w_in.astype(jnp.float32)) + b_in
        hidden = jax.nn.silu(pre_act).astype(jnp.bfloat16)
        predicted = jnp.einsum('mdkh,hv->mdkv', hidden.astype(jnp.float32), w_out.astype(jnp.float32)) + b_out
        target = jnp.take(obs_value, owner_index, axis=1)
        live = jnp.take(live_mask, owner_index, axis=1)
        return (weights, picked_ids, pre_act, predicted, target, live)

    def loss_piece(owner_index):
        outputs = forward(owner_index)
        predicted, target, live = (outputs[3], outputs[4], outputs[5])
        obs_diff = predicted - target[None]
        pair_diff = predicted[:, None] - predicted[None, :]
        per_obs = lax.optimization_barrier(jnp.sum(smooth_abs(obs_diff), axis=0)) / MEMBERS - lax.optimization_barrier(jnp.sum(smooth_abs(pair_diff), axis=(0, 1))) / (2.0 * MEMBERS * (MEMBERS - 1))
        return jnp.sum(per_obs * live[:, :, None])
    loss_sum = jnp.sum(lax.map(loss_piece, owners))
    live_total = jnp.sum(live_mask)
    loss_value = loss_sum / (OBS_CH * live_total)
    grad_scale = OBS_ALL / live_total

    def grad_piece(owner_index):
        weights, picked_ids, pre_act, predicted, target, live = forward(owner_index)
        obs_diff = predicted - target[None]
        pair_diff = predicted[:, None] - predicted[None, :]
        slope_obs = obs_diff / smooth_abs(obs_diff)
        slope_pair = lax.optimization_barrier(jnp.sum(pair_diff / smooth_abs(pair_diff), axis=1))
        grad_pred = (grad_scale * live[None, :, :, None] * (slope_obs / MEMBERS - slope_pair / (MEMBERS * (MEMBERS - 1.0)))).astype(jnp.bfloat16)
        grad_hidden = jnp.einsum('mdkv,hv->mdkh', grad_pred.astype(jnp.float32), w_out.astype(jnp.float32))
        grad_act = (grad_hidden * silu_slope(pre_act)).astype(jnp.bfloat16)
        grad_interp = jnp.einsum('mdkh,ch->mdkc', grad_act.astype(jnp.float32), w_in.astype(jnp.float32)).astype(jnp.bfloat16)
        contribution = jnp.einsum('dkp,mdkc->mdpc', weights.astype(jnp.float32), grad_interp.astype(jnp.float32)).astype(jnp.bfloat16)
        block_onehot = (picked_ids[:, None] == jnp.arange(block_count, dtype=jnp.int32)[None, :]).astype(jnp.float32)
        return jnp.einsum('mdpc,db->mbpc', contribution.astype(jnp.float32), block_onehot)
    grads = lax.map(grad_piece, owners)
    latent_grad = jnp.transpose(grads, (1, 0, 2, 3, 4)).reshape(MEMBERS, POINTS, WIDTH)
    return (latent_grad, loss_value)
```

```python
import jax
import jax.numpy as jnp
from jax import lax
from jax.sharding import PartitionSpec as P

SOFTEN = 0.1


def smooth_abs(value):
    return jnp.sqrt(value * value + SOFTEN * SOFTEN)


def silu_slope(pre_act):
    sigmoid_value = jax.nn.sigmoid(pre_act)
    return sigmoid_value * (1.0 + pre_act * (1.0 - sigmoid_value))


def per_device(latent, block_pick, obs_weight, obs_value, obs_count, w_in, b_in, w_out, b_out):
    members_here, points, feature_width = latent.shape
    peer_count = lax.axis_size("grid")
    slot_count = obs_weight.shape[2]
    block_size = obs_weight.shape[3]
    channels = obs_value.shape[3]
    members_all = members_here * lax.axis_size("member")
    block_count = points // block_size
    local_blocks = latent.reshape(members_here, block_count, block_size, feature_width)
    picked_ids = block_pick[0]
    block_onehot = (
        picked_ids[:, None] == jnp.arange(block_count, dtype=jnp.int32)[None, :]
    ).astype(jnp.bfloat16)
    weights_here = lax.all_to_all(obs_weight[0], "grid", split_axis=0, concat_axis=0, tiled=True)
    target = lax.all_to_all(obs_value[0], "grid", split_axis=0, concat_axis=0, tiled=True)
    counts = lax.all_gather(obs_count[0], "grid", axis=0)
    counts_here = lax.dynamic_index_in_dim(counts, lax.axis_index("grid"), axis=1, keepdims=False)
    weight_sum = jnp.sum(weights_here, axis=2, keepdims=True, dtype=jnp.float32)
    norm_weight = (weights_here / weight_sum).astype(jnp.bfloat16)
    picked = local_blocks[:, picked_ids]
    interp = jnp.einsum(
        "jkp,mjpc->mjkc", norm_weight, picked, preferred_element_type=jnp.float32
    ).astype(jnp.bfloat16)
    flat_rows = interp.reshape(members_here * peer_count * slot_count, feature_width)
    pre_act = jnp.dot(flat_rows, w_in, preferred_element_type=jnp.float32) + b_in
    hidden = jax.nn.silu(pre_act).astype(jnp.bfloat16)
    predicted = jnp.dot(hidden, w_out, preferred_element_type=jnp.float32) + b_out
    predicted = predicted.reshape(members_here, peer_count, slot_count, channels)
    all_members = lax.all_gather(predicted, "member", axis=0, tiled=True)
    live_mask = (jnp.arange(slot_count, dtype=jnp.int32)[None, :] < counts_here[:, None]).astype(
        jnp.float32
    )
    obs_diff = predicted - target[None]
    pair_diff = predicted[:, None] - all_members[None]
    per_obs = smooth_abs(obs_diff) / members_all - jnp.sum(smooth_abs(pair_diff), axis=1) / (
        2.0 * members_all * (members_all - 1)
    )
    loss_part = jnp.sum(per_obs * live_mask[None, :, :, None])
    live_total = jnp.sum(counts).astype(jnp.float32)
    loss_total = lax.psum(loss_part, ("member", "grid"))
    loss_value = loss_total / (channels * live_total)
    grad_scale = peer_count * peer_count * slot_count / live_total
    slope_obs = obs_diff / smooth_abs(obs_diff)
    slope_pair = jnp.sum(pair_diff / smooth_abs(pair_diff), axis=1)
    grad_pred = (
        grad_scale
        * live_mask[None, :, :, None]
        * (slope_obs / members_all - slope_pair / (members_all * (members_all - 1.0)))
    ).astype(jnp.bfloat16)
    grad_hidden = jnp.einsum(
        "rv,hv->rh", grad_pred.reshape(-1, channels), w_out, preferred_element_type=jnp.float32
    )
    grad_act = (grad_hidden * silu_slope(pre_act)).astype(jnp.bfloat16)
    grad_interp = jnp.einsum(
        "rh,ch->rc", grad_act, w_in, preferred_element_type=jnp.float32
    ).astype(jnp.bfloat16)
    grad_interp = grad_interp.reshape(members_here, peer_count, slot_count, feature_width)
    contribution = jnp.einsum(
        "jkp,mjkc->mjpc", norm_weight, grad_interp, preferred_element_type=jnp.float32
    ).astype(jnp.bfloat16)
    summed = jnp.einsum("mdpc,db->mbpc", contribution, block_onehot, preferred_element_type=jnp.float32)
    latent_grad = summed.reshape(members_here, points, feature_width)
    return (latent_grad, loss_value)


def solution(mesh):
    in_specs = (
        P("member", "grid", None),
        P("grid", None),
        P("grid", None, None, None),
        P("grid", None, None, None),
        P("grid", None),
        P(),
        P(),
        P(),
        P(),
    )
    out_specs = (P("member", "grid", None), P())
    return jax.shard_map(
        per_device, mesh=mesh, in_specs=in_specs, out_specs=out_specs, check_vma=False
    )
```

```python
import functools

import jax
import jax.numpy as jnp
from jax import lax
from jax.experimental import pallas as pl
from jax.experimental.pallas import tpu as pltpu
from jax.sharding import PartitionSpec as P

SOFTEN = 0.1
F32 = jnp.float32
BF16 = jnp.bfloat16
NT = (((1,), (1,)), ((), ()))


def root_terms(value):
    square = value * value + SOFTEN * SOFTEN
    inverse = lax.rsqrt(square)
    return square * inverse, value * inverse


def network_kernel(
    n, picks, count_in, b_in, w_in, w_out, b_out, w_hbm, o_hbm, lat_hbm,
    contrib_out, loss_out,
    lat, wbuf, obuf, cbuf, wt, slope, preds, peers, gpred, contrib, acc, lbuf,
    sems, lsems, osems,
):
    core = lax.axis_index("member")
    me = lax.axis_index("grid")
    other = 1 - core
    members = lat.shape[0]
    slots, block = wbuf.shape[1] * wbuf.shape[2], wbuf.shape[3]
    channels = obuf.shape[3]
    rows = members * slots
    members_all = 2 * members

    def remote(src, dst, kind, s, target):
        return pltpu.make_async_remote_copy(
            src_ref=src, dst_ref=dst, send_sem=sems.at[kind, s], recv_sem=sems.at[kind + 1, s],
            device_id=target, device_id_type=pl.DeviceIdType.MESH)

    def peer(s):
        return lax.rem(me + s, n)

    def w_copy(s):
        return remote(w_hbm.at[peer(s), core], wbuf.at[s, core], 0, s, (core, peer(s)))

    def o_copy(s):
        return remote(o_hbm.at[peer(s), core], obuf.at[s, core], 2, s, (core, peer(s)))

    def c_copy(s):
        return remote(count_in, cbuf.at[s], 4, s, (core, peer(s)))

    def fw_copy(s, half):
        return remote(wbuf.at[s, half], wbuf.at[s, half], 6, s, (other, me))

    def fo_copy(s, half):
        return remote(obuf.at[s, half], obuf.at[s, half], 8, s, (other, me))

    def p_copy(s):
        return remote(preds.at[s], peers.at[s], 10, s, (other, me))

    def l_copy(s):
        return remote(acc.at[2], lbuf.at[me], 12, s, (core, peer(s)))

    def l_land(s):
        source = lax.rem(me - s + n, n)
        return remote(acc.at[2], lbuf.at[source], 12, s, (core, source))

    lat_copy = pltpu.make_async_copy(lat_hbm, lat, lsems.at[0])
    own_w = pltpu.make_async_copy(w_hbm.at[me], wbuf.at[0], lsems.at[1])
    own_o = pltpu.make_async_copy(o_hbm.at[me], obuf.at[0], lsems.at[2])
    acc_copy = pltpu.make_async_remote_copy(
        src_ref=acc.at[0], dst_ref=acc.at[1], send_sem=lsems.at[3], recv_sem=lsems.at[4],
        device_id=(other, me), device_id_type=pl.DeviceIdType.MESH)
    own_w.start()
    lat_copy.start()
    own_o.start()

    barrier = pltpu.get_barrier_semaphore()
    pl.semaphore_signal(barrier, inc=1, device_id=(other, me), device_id_type=pl.DeviceIdType.MESH)

    @pl.loop(1, n)
    def _(s):
        pl.semaphore_signal(
            barrier, inc=1, device_id=(core, peer(s)), device_id_type=pl.DeviceIdType.MESH)

    pl.semaphore_wait(barrier, n)

    @pl.loop(1, n)
    def _(s):
        c_copy(s).start()

    @pl.loop(1, n)
    def _(s):
        w_copy(s).start()
        o_copy(s).start()

    cbuf[0] = count_in[...]
    acc[0] = jnp.zeros(acc.shape[1:], F32)

    def pass_on(s):
        w_copy(s).wait_recv()
        fw_copy(s, core).start()
        o_copy(s).wait_recv()
        fo_copy(s, core).start()

    def forward(s):
        source = lax.rem(me - s + n, n)
        pick = picks[0, source]
        raw = wbuf[s].reshape(slots, block).astype(F32)
        norm = raw / jnp.sum(raw, axis=1, keepdims=True)
        wt[s] = norm.T.astype(BF16)
        norm = norm.astype(BF16)
        interp = jnp.concatenate([
            jnp.dot(norm, lat[m, pick], preferred_element_type=F32).astype(BF16)
            for m in range(members)], axis=0)
        pre = jnp.dot(interp, w_in[...], preferred_element_type=F32) + b_in[...]
        gate = 0.5 * jnp.tanh(0.5 * pre) + 0.5
        slope[s] = gate * (1.0 + pre * (1.0 - gate))
        hidden = (pre * gate).astype(BF16)
        preds[s] = jnp.dot(hidden, w_out[...], preferred_element_type=F32) + b_out[...]
        p_copy(s).start()

    def counts_total():
        def add(s, total):
            return total + cbuf[s, 0:1, :]
        return jnp.sum(lax.fori_loop(1, n, add, cbuf[0, 0:1, :]), axis=1, keepdims=True)

    def losses(s, scale):
        p_copy(s).wait_recv()
        lane = lax.broadcasted_iota(jnp.int32, (1, cbuf.shape[2]), 1)
        count = jnp.sum(jnp.where(lane == me, cbuf[s, 0:1, :], 0.0), axis=1, keepdims=True)
        slot = lax.broadcasted_iota(jnp.int32, (slots, channels), 0).astype(F32)
        live = slot < count
        target = obuf[s].reshape(slots, channels)
        mine = [preds[s, m * slots:(m + 1) * slots, :] for m in range(members)]
        theirs = [peers[s, m * slots:(m + 1) * slots, :] for m in range(members)]
        near = jnp.zeros((slots, channels), F32)
        pairs = jnp.full((slots, channels), members * SOFTEN, F32)
        slope_obs = []
        slope_pair = [jnp.zeros((slots, channels), F32) for _ in range(members)]
        for i in range(members):
            size, sign = root_terms(mine[i] - target)
            near = near + size
            slope_obs.append(sign)
            for i2 in range(i + 1, members):
                size, sign = root_terms(mine[i] - mine[i2])
                pairs = pairs + 2.0 * size
                slope_pair[i] = slope_pair[i] + sign
                slope_pair[i2] = slope_pair[i2] - sign
            for i2 in range(members):
                size, sign = root_terms(mine[i] - theirs[i2])
                pairs = pairs + size
                slope_pair[i] = slope_pair[i] + sign
        per_obs = near * (1.0 / members_all) - pairs * (1.0 / (2.0 * members_all * (members_all - 1)))
        per_obs = jnp.where(live, per_obs, 0.0)
        acc[0] = acc[0] + jnp.sum(per_obs.reshape(slots // 8, 8, channels), axis=0)
        factor = jnp.where(live, scale, 0.0)
        for i in range(members):
            grad = factor * (slope_obs[i] * (1.0 / members_all)
                             - slope_pair[i] * (1.0 / (members_all * (members_all - 1.0))))
            gpred[s, i * slots:(i + 1) * slots, :] = grad.astype(BF16)

    def backward(s):
        grad_hidden = lax.dot_general(gpred[s], w_out[...], NT, preferred_element_type=F32)
        grad_act = (grad_hidden * slope[s]).astype(BF16)
        grad_interp = lax.dot_general(
            grad_act, w_in[...], NT, preferred_element_type=F32).astype(BF16)
        for m in range(members):
            contrib[s, m] = jnp.dot(
                wt[s], grad_interp[m * slots:(m + 1) * slots, :],
                preferred_element_type=F32).astype(BF16)
        pltpu.make_async_copy(contrib.at[s], contrib_out.at[s], osems.at[s]).start()

    own_w.wait()
    lat_copy.wait()
    own_o.wait()
    forward(0)
    if n > 1:
        pass_on(1)

    @pl.loop(1, n)
    def _(s):
        c_copy(s).wait_recv()

    total = counts_total()
    scale = (n * n * slots) / total

    @pl.loop(1, n)
    def _(s):
        @pl.when(s + 1 < n)
        def _():
            pass_on(s + 1)

        fw_copy(s, other).wait_recv()
        fo_copy(s, other).wait_recv()
        forward(s)
        losses(s - 1, scale)

    losses(n - 1, scale)
    acc_copy.start()
    backward(0)
    acc_copy.wait()
    acc[2] = acc[0] + acc[1]
    lbuf[me] = acc[0] + acc[1]

    @pl.loop(1, n)
    def _(s):
        l_copy(s).start()

    @pl.loop(1, n)
    def _(s):
        backward(s)

    @pl.loop(1, n)
    def _(s):
        l_land(s).wait_recv()

    def add_loss(s, so_far):
        return so_far + lbuf[s]

    loss = lax.fori_loop(1, n, add_loss, lbuf[0])
    loss_out[...] = jnp.broadcast_to(
        jnp.sum(jnp.sum(loss, axis=0, keepdims=True), axis=1, keepdims=True) / (channels * total),
        loss_out.shape)
    p_copy(0).wait_send()

    @pl.loop(1, n)
    def _(s):
        w_copy(s).wait_send()
        o_copy(s).wait_send()
        c_copy(s).wait_send()
        fw_copy(s, core).wait_send()
        fo_copy(s, core).wait_send()
        p_copy(s).wait_send()
        l_copy(s).wait_send()

    @pl.loop(0, n)
    def _(s):
        pltpu.make_async_copy(contrib.at[s], contrib_out.at[s], osems.at[s]).wait()


def scatter_kernel(n, picks, contrib, loss_in, out, loss_out):
    me = lax.axis_index("grid")
    b = pl.program_id(0)
    loss_out[...] = loss_in[...]
    out[...] = jnp.zeros_like(out)

    @pl.loop(0, n)
    def _(s):
        @pl.when(picks[0, lax.rem(me - s + n, n)] == b)
        def _():
            for m in range(out.shape[0]):
                out[m] = out[m] + contrib[s, m].astype(F32)


def per_device(latent, block_pick, obs_weight, obs_value, obs_count, w_in, b_in, w_out, b_out):
    members, points, width = latent.shape
    n = lax.axis_size("grid")
    slots, block = obs_weight.shape[2:]
    channels = obs_value.shape[3]
    inner = w_in.shape[1]
    blocks = points // block
    lanes = -(-n // 128) * 128
    rows = members * slots
    counts = jnp.pad(obs_count.astype(F32), ((0, 7), (0, lanes - n)))
    weights = obs_weight.reshape(n, 2, slots // 2, block)
    values = obs_value.reshape(n, 2, slots // 2, channels)
    vmem = pl.BlockSpec(memory_space=pltpu.VMEM)
    smem = pl.BlockSpec(memory_space=pltpu.SMEM)
    anywhere = pl.BlockSpec(memory_space=pl.ANY)
    contrib, loss = pl.pallas_call(
        functools.partial(network_kernel, n),
        out_shape=(
            jax.ShapeDtypeStruct((n, members, block, width), BF16),
            jax.ShapeDtypeStruct((8, 128), F32),
        ),
        in_specs=[smem] + [vmem] * 5 + [anywhere] * 3,
        out_specs=(anywhere, vmem),
        scratch_shapes=[
            pltpu.VMEM((members, blocks, block, width), BF16),
            pltpu.VMEM((n, 2, slots // 2, block), BF16),
            pltpu.VMEM((n, 2, slots // 2, channels), F32),
            pltpu.VMEM((n, 8, lanes), F32),
            pltpu.VMEM((n, block, slots), BF16),
            pltpu.VMEM((n, rows, inner), F32),
            pltpu.VMEM((n, rows, channels), F32),
            pltpu.VMEM((n, rows, channels), F32),
            pltpu.VMEM((n, rows, channels), BF16),
            pltpu.VMEM((n, members, block, width), BF16),
            pltpu.VMEM((3, 8, channels), F32),
            pltpu.VMEM((n, 8, channels), F32),
            pltpu.SemaphoreType.DMA((14, n)),
            pltpu.SemaphoreType.DMA((5,)),
            pltpu.SemaphoreType.DMA((n,)),
        ],
        compiler_params=pltpu.CompilerParams(
            collective_id=0, has_side_effects=True, vmem_limit_bytes=56 * 1024 * 1024),
        name="network",
    )(block_pick, counts, b_in.reshape(1, -1), w_in, w_out, b_out.reshape(1, -1),
      weights, values, latent.reshape(members, blocks, block, width))
    grad, loss = pl.pallas_call(
        functools.partial(scatter_kernel, n),
        out_shape=(
            jax.ShapeDtypeStruct((members, points, width), F32),
            jax.ShapeDtypeStruct((8, 128), F32),
        ),
        grid=(blocks,),
        in_specs=[smem, pl.BlockSpec((n, members, block, width), lambda b: (0, 0, 0, 0)),
                  pl.BlockSpec((8, 128), lambda b: (0, 0))],
        out_specs=(pl.BlockSpec((members, block, width), lambda b: (0, b, 0)),
                   pl.BlockSpec((8, 128), lambda b: (0, 0))),
        compiler_params=pltpu.CompilerParams(vmem_limit_bytes=32 * 1024 * 1024),
        name="scatter",
    )(block_pick, contrib, loss)
    return (grad, loss[0, 0])


def solution(mesh):
    in_specs = (
        P("member", "grid", None),
        P("grid", None),
        P("grid", None, None, None),
        P("grid", None, None, None),
        P("grid", None),
        P(),
        P(),
        P(),
        P(),
    )
    out_specs = (P("member", "grid", None), P())
    return jax.shard_map(
        per_device, mesh=mesh, in_specs=in_specs, out_specs=out_specs, check_vma=False
    )
```

```python
import functools

import jax
import jax.numpy as jnp
from jax import lax
from jax.experimental import pallas as pl
from jax.experimental.pallas import tpu as pltpu
from jax.sharding import PartitionSpec as P

SOFTEN = 0.1
LOSS_LAG = 2
F32 = jnp.float32
BF16 = jnp.bfloat16
NT = (((1,), (1,)), ((), ()))


def root_terms(value):
    square = value * value + SOFTEN * SOFTEN
    inverse = lax.rsqrt(square)
    return square * inverse, value * inverse


def network_kernel(
    n, picks, count_in, b_in, w_in, w_out, b_out, w_hbm, o_hbm, lat_hbm,
    contrib_out, loss_out,
    lat, wbuf, obuf, cbuf, wt, slope, preds, peers, gpred, contrib, acc, lbuf,
    sems, lsems, osems,
):
    core = lax.axis_index("member")
    me = lax.axis_index("grid")
    other = 1 - core
    members = lat.shape[0]
    slots, block = wbuf.shape[1] * wbuf.shape[2], wbuf.shape[3]
    channels = obuf.shape[3]
    rows = members * slots
    members_all = 2 * members

    def remote(src, dst, kind, s, target):
        return pltpu.make_async_remote_copy(
            src_ref=src, dst_ref=dst, send_sem=sems.at[kind, s], recv_sem=sems.at[kind + 1, s],
            device_id=target, device_id_type=pl.DeviceIdType.MESH)

    def peer(s):
        return lax.rem(me + s, n)

    def source_of(s):
        return lax.rem(me - s + n, n)

    def w_copy(s):
        return remote(w_hbm.at[peer(s), core], wbuf.at[s, core], 0, s, (core, peer(s)))

    def o_copy(s):
        return remote(o_hbm.at[peer(s), core], obuf.at[s, core], 2, s, (core, peer(s)))

    def c_copy(s):
        return remote(count_in, cbuf.at[s], 4, s, (core, peer(s)))

    def fw_copy(s, half):
        return remote(wbuf.at[s, half], wbuf.at[s, half], 6, s, (other, me))

    def fo_copy(s, half):
        return remote(obuf.at[s, half], obuf.at[s, half], 8, s, (other, me))

    def p_copy(s):
        return remote(preds.at[s], peers.at[s], 10, s, (other, me))

    def l_copy(s):
        return remote(acc.at[2], lbuf.at[me], 12, s, (core, peer(s)))

    def l_land(s):
        source = source_of(s)
        return remote(acc.at[2], lbuf.at[source], 12, s, (core, source))

    lat_copy = pltpu.make_async_copy(lat_hbm, lat, lsems.at[0])
    own_w = pltpu.make_async_copy(w_hbm.at[me], wbuf.at[0], lsems.at[1])
    own_o = pltpu.make_async_copy(o_hbm.at[me], obuf.at[0], lsems.at[2])
    acc_copy = pltpu.make_async_remote_copy(
        src_ref=acc.at[0], dst_ref=acc.at[1], send_sem=lsems.at[3], recv_sem=lsems.at[4],
        device_id=(other, me), device_id_type=pl.DeviceIdType.MESH)
    own_w.start()
    lat_copy.start()
    own_o.start()

    barrier = pltpu.get_barrier_semaphore()
    pl.semaphore_signal(barrier, inc=1, device_id=(other, me), device_id_type=pl.DeviceIdType.MESH)

    @pl.loop(1, n)
    def _(s):
        pl.semaphore_signal(
            barrier, inc=1, device_id=(core, peer(s)), device_id_type=pl.DeviceIdType.MESH)

    pl.semaphore_wait(barrier, n)

    @pl.loop(1, n)
    def _(s):
        c_copy(s).start()

    @pl.loop(1, n)
    def _(s):
        w_copy(s).start()
        o_copy(s).start()

    cbuf[0] = count_in[...]
    acc[0] = jnp.zeros(acc.shape[1:], F32)

    def pass_on(s):
        w_copy(s).wait_recv()
        fw_copy(s, core).start()
        o_copy(s).wait_recv()
        fo_copy(s, core).start()

    def forward(s):
        pick = picks[0, source_of(s)]
        raw = wbuf[s].reshape(slots, block).astype(F32)
        norm = raw / jnp.sum(raw, axis=1, keepdims=True)
        wt[s] = norm.T.astype(BF16)
        norm = norm.astype(BF16)
        interp = jnp.concatenate([
            jnp.dot(norm, lat[m, pick], preferred_element_type=F32).astype(BF16)
            for m in range(members)], axis=0)
        pre = jnp.dot(interp, w_in[...], preferred_element_type=F32) + b_in[...]
        gate = 0.5 * jnp.tanh(0.5 * pre) + 0.5
        slope[s] = gate * (1.0 + pre * (1.0 - gate))
        hidden = (pre * gate).astype(BF16)
        preds[s] = jnp.dot(hidden, w_out[...], preferred_element_type=F32) + b_out[...]

    def counts_total():
        def add(s, total):
            return total + cbuf[s]
        counts = lax.fori_loop(1, n, add, cbuf[0])
        return jnp.sum(counts.astype(F32), axis=1, keepdims=True)

    def losses(s, scale):
        lane = lax.broadcasted_iota(jnp.int32, (1, cbuf.shape[2]), 1)
        count = jnp.sum(
            jnp.where(lane == me, cbuf[s].astype(F32), 0.0), axis=1, keepdims=True)
        slot = lax.broadcasted_iota(jnp.int32, (slots, channels), 0).astype(F32)
        live = slot < count
        target = obuf[s].reshape(slots, channels)
        mine = [preds[s, m * slots:(m + 1) * slots, :] for m in range(members)]
        theirs = [peers[s, m * slots:(m + 1) * slots, :] for m in range(members)]
        near = jnp.zeros((slots, channels), F32)
        pairs = jnp.full((slots, channels), members * SOFTEN, F32)
        slope_obs = []
        slope_pair = [jnp.zeros((slots, channels), F32) for _ in range(members)]
        for i in range(members):
            size, sign = root_terms(mine[i] - target)
            near = near + size
            slope_obs.append(sign)
            for i2 in range(i + 1, members):
                size, sign = root_terms(mine[i] - mine[i2])
                pairs = pairs + 2.0 * size
                slope_pair[i] = slope_pair[i] + sign
                slope_pair[i2] = slope_pair[i2] - sign
            for i2 in range(members):
                size, sign = root_terms(mine[i] - theirs[i2])
                pairs = pairs + size
                slope_pair[i] = slope_pair[i] + sign
        per_obs = near * (1.0 / members_all) - pairs * (1.0 / (2.0 * members_all * (members_all - 1)))
        per_obs = jnp.where(live, per_obs, 0.0)
        acc[0] = acc[0] + jnp.sum(per_obs.reshape(slots // 8, 8, channels), axis=0)
        factor = jnp.where(live, scale, 0.0)
        for i in range(members):
            grad = factor * (slope_obs[i] * (1.0 / members_all)
                             - slope_pair[i] * (1.0 / (members_all * (members_all - 1.0))))
            gpred[s, i * slots:(i + 1) * slots, :] = grad.astype(BF16)

    def backward(s):
        grad_hidden = lax.dot_general(gpred[s], w_out[...], NT, preferred_element_type=F32)
        grad_act = (grad_hidden * slope[s]).astype(BF16)
        grad_interp = lax.dot_general(
            grad_act, w_in[...], NT, preferred_element_type=F32).astype(BF16)
        for m in range(members):
            contrib[s, m] = jnp.dot(
                wt[s], grad_interp[m * slots:(m + 1) * slots, :],
                preferred_element_type=F32).astype(BF16)

    def give(s):
        pltpu.make_async_copy(contrib.at[s], contrib_out.at[s], osems.at[s]).start()

    own_w.wait()
    lat_copy.wait()
    own_o.wait()
    wait = min(LOSS_LAG, n - 1)
    forward(0)
    p_copy(0).start()
    if n > 1:
        pass_on(1)

    @pl.loop(1, n)
    def _(s):
        c_copy(s).wait_recv()

    total = counts_total()
    scale = (n * n * slots) / total

    def ready(s):
        @pl.when(s + 1 < n)
        def _():
            pass_on(s + 1)

        fw_copy(s, other).wait_recv()
        fo_copy(s, other).wait_recv()

    @pl.loop(1, wait)
    def _(s):
        ready(s)
        forward(s)
        p_copy(s).start()

    @pl.loop(wait, n)
    def _(s):
        ready(s)
        p_copy(s - wait).wait_recv()
        losses(s - wait, scale)
        forward(s)
        p_copy(s).start()

    @pl.loop(n - wait, n)
    def _(s):
        p_copy(s).wait_recv()
        losses(s, scale)

    acc_copy.start()
    middle = min(2, n)

    @pl.loop(0, middle)
    def _(s):
        backward(s)
        give(s)

    acc_copy.wait()
    acc[2] = acc[0] + acc[1]
    lbuf[me] = acc[0] + acc[1]

    @pl.loop(1, n)
    def _(s):
        l_copy(s).start()

    @pl.loop(middle, n)
    def _(s):
        backward(s)
        give(s)

    @pl.loop(1, n)
    def _(s):
        l_land(s).wait_recv()

    def add_loss(s, so_far):
        return so_far + lbuf[s]

    loss = lax.fori_loop(1, n, add_loss, lbuf[0])
    loss = jnp.sum(loss / (channels * total))
    loss_out[0, 0] = loss
    p_copy(0).wait_send()

    @pl.loop(1, n)
    def _(s):
        w_copy(s).wait_send()
        o_copy(s).wait_send()
        c_copy(s).wait_send()
        fw_copy(s, core).wait_send()
        fo_copy(s, core).wait_send()
        p_copy(s).wait_send()
        l_copy(s).wait_send()

    @pl.loop(0, n)
    def _(s):
        pltpu.make_async_copy(contrib.at[s], contrib_out.at[s], osems.at[s]).wait()


def scatter_kernel(n, picks, contrib, loss_in, out, loss_out):
    me = lax.axis_index("grid")
    members, block = contrib.shape[1:3]
    here = out.shape[1] // block
    first = pl.program_id(0) * here
    loss_out[0, 0] = loss_in[0, 0]
    out[...] = jnp.zeros_like(out)

    @pl.loop(0, n)
    def _(s):
        place = picks[0, lax.rem(me - s + n, n)] - first

        @pl.when((place >= 0) & (place < here))
        def _():
            rows = pl.ds(pl.multiple_of(place * block, block), block)
            for m in range(members):
                out[m, rows, :] = out[m, rows, :] + contrib[s, m].astype(F32)


def per_device(latent, block_pick, obs_weight, obs_value, obs_count, w_in, b_in, w_out, b_out):
    members, points, width = latent.shape
    n = lax.axis_size("grid")
    slots, block = obs_weight.shape[2:]
    channels = obs_value.shape[3]
    inner = w_in.shape[1]
    blocks = points // block
    rows = members * slots
    weights = obs_weight.reshape(n, 2, slots // 2, block)
    values = obs_value.reshape(n, 2, slots // 2, channels)
    vmem = pl.BlockSpec(memory_space=pltpu.VMEM)
    smem = pl.BlockSpec(memory_space=pltpu.SMEM)
    anywhere = pl.BlockSpec(memory_space=pl.ANY)
    contrib, loss = pl.pallas_call(
        functools.partial(network_kernel, n),
        out_shape=(
            jax.ShapeDtypeStruct((n, members, block, width), BF16),
            jax.ShapeDtypeStruct((1, 1), F32),
        ),
        in_specs=[smem] + [vmem] * 5 + [anywhere] * 3,
        out_specs=(anywhere, smem),
        scratch_shapes=[
            pltpu.VMEM((members, blocks, block, width), BF16),
            pltpu.VMEM((n, 2, slots // 2, block), BF16),
            pltpu.VMEM((n, 2, slots // 2, channels), F32),
            pltpu.VMEM((n, 1, n), jnp.int32),
            pltpu.VMEM((n, block, slots), BF16),
            pltpu.VMEM((n, rows, inner), F32),
            pltpu.VMEM((n, rows, channels), F32),
            pltpu.VMEM((n, rows, channels), F32),
            pltpu.VMEM((n, rows, channels), BF16),
            pltpu.VMEM((n, members, block, width), BF16),
            pltpu.VMEM((3, 8, channels), F32),
            pltpu.VMEM((n, 8, channels), F32),
            pltpu.SemaphoreType.DMA((14, n)),
            pltpu.SemaphoreType.DMA((5,)),
            pltpu.SemaphoreType.DMA((n,)),
        ],
        compiler_params=pltpu.CompilerParams(
            collective_id=0, has_side_effects=True, vmem_limit_bytes=56 * 1024 * 1024),
        name="network",
    )(block_pick, obs_count, b_in.reshape(1, -1), w_in, w_out, b_out.reshape(1, -1),
      weights, values, latent.reshape(members, blocks, block, width))
    steps = 4 if blocks % 4 == 0 else 1
    grad, loss = pl.pallas_call(
        functools.partial(scatter_kernel, n),
        out_shape=(
            jax.ShapeDtypeStruct((members, points, width), F32),
            jax.ShapeDtypeStruct((1, 1), F32),
        ),
        grid=(steps,),
        in_specs=[smem, pl.BlockSpec((n, members, block, width), lambda b: (0, 0, 0, 0)),
                  smem],
        out_specs=(pl.BlockSpec((members, points // steps, width), lambda b: (0, b, 0)), smem),
        compiler_params=pltpu.CompilerParams(vmem_limit_bytes=32 * 1024 * 1024),
        name="scatter",
    )(block_pick, contrib, loss)
    return (grad, loss.reshape(()))


def solution(mesh):
    in_specs = (
        P("member", "grid", None),
        P("grid", None),
        P("grid", None, None, None),
        P("grid", None, None, None),
        P("grid", None),
        P(),
        P(),
        P(),
        P(),
    )
    out_specs = (P("member", "grid", None), P())
    return jax.shard_map(
        per_device, mesh=mesh, in_specs=in_specs, out_specs=out_specs, check_vma=False
    )
```
